32 devices in a mesh: row: 4 (over y, x), col: 8 (over z, core).
Axes of the slice: x: 2, y: 2, z: 4, core: 2. Of those that a mesh axis runs over, the one named last changes fastest.
Arguments:
- tokens: bfloat16 [1024, 6144], P('col', 'row'), may hold values from -6 to 6
- learning_rate: float32 [1], replicated, may hold values from 0.05 to 0.5
- weight_in: bfloat16 [6144, 24576], P('row', 'col'), may hold values from -0.078125 to 0.078125
- grad_in: bfloat16 [6144, 24576], P('row', 'col'), may hold values from -6 to 6
- moment_in: bfloat16 [6144, 24576], P('row', 'col'), may hold values from -4 to 4
- second_in: bfloat16 [6144, 24576], P('row', 'col'), may hold values from 0.25 to 4
- weight_out: bfloat16 [24576, 6144], P('col', 'row'), may hold values from -0.0390625 to 0.0390625
- grad_out: bfloat16 [24576, 6144], P('col', 'row'), may hold values from -6 to 6
- moment_out: bfloat16 [24576, 6144], P('col', 'row'), may hold values from -4 to 4
- second_out: bfloat16 [24576, 6144], P('col', 'row'), may hold values from 0.25 to 4
Outputs:
- block_out: bfloat16 [1024, 6144], P('col', 'row')
- block_tangent: bfloat16 [1024, 6144], P('col', 'row')
The draws below stay inside these ranges and needn't reach their ends.
All inputs are finite; a program needn't handle non-finite values.
Results may differ from the reference program's by a relative error of at most 0.025.
Values may be sent and summed in bfloat16 or wider, within the bound.
A program may use at most 192 MiB of HBM per device.

```python
import math
import jax
import jax.numpy as jnp
from jax import lax

D = 6144
FF = 24576
TOKENS = 1024
N_ROW = 4
N_COL = 8


def shard_levels(stream_key, shape, cuts, low, largest):
    def one(dim, blocks):
        draws = jax.random.uniform(jax.random.fold_in(jax.random.fold_in(stream_key, 6), dim), (blocks,), jnp.float32, low / len(cuts), largest / len(cuts))
        return jnp.repeat(jnp.exp(draws), shape[dim] // blocks).reshape((-1,) + (1,) * (len(shape) - dim - 1))

    gain = one(*cuts[0])
    for cut in cuts[1:]:
        gain = gain * one(*cut)
    return gain


def scatter_about(own_key, dims, scale, most, cuts=(), kind=jnp.bfloat16):
    result = jax.random.normal(own_key, dims, jnp.float32) * scale
    if len(cuts) > 0:
        result = shard_levels(own_key, dims, cuts, -0.22, 0.18) * result
    return jnp.clip(result, min=-most, max=most).astype(kind)


def setup_inputs(seed: int = 0) -> dict:
    splits = jax.random.split(jax.random.key(seed), 11)
    tokens = scatter_about(splits[0], (TOKENS, D), 1.0, 6.0, ((0, 8), (1, 4)))
    learning_rate = jnp.clip(jnp.exp(jax.random.uniform(splits[1], (1,), jnp.float32, math.log(0.05), math.log(0.5))), 0.05, 0.5)
    weight_in = scatter_about(splits[2], (D, FF), D ** -0.5, 0.078125, ((0, 4), (1, 8)))
    grad_in = scatter_about(splits[3], (D, FF), 1.0, 6.0, ((0, 4), (1, 8)))
    moment_in = scatter_about(splits[4], (D, FF), 0.5, 4.0, ((0, 4), (1, 8)))
    second_in = jnp.clip(jnp.exp(math.log(4.0) - 2.7725887 * jax.random.uniform(splits[5], (D, FF), jnp.float32) ** shard_levels(splits[5], (D, FF), ((0, 4), (1, 8)), -0.2, 0.2)), 0.25, 4.0).astype(jnp.bfloat16)
    weight_out = scatter_about(splits[6], (FF, D), FF ** -0.5, 0.0390625, ((0, 8), (1, 4)))
    grad_out = scatter_about(splits[7], (FF, D), 1.0, 6.0, ((0, 8), (1, 4)))
    moment_out = scatter_about(splits[8], (FF, D), 0.5, 4.0, ((0, 8), (1, 4)))
    second_out = jnp.clip(jnp.exp(math.log(4.0) - 2.7725887 * jax.random.uniform(splits[9], (FF, D), jnp.float32) ** shard_levels(splits[9], (FF, D), ((0, 8), (1, 4)), -0.2, 0.2)), 0.25, 4.0).astype(jnp.bfloat16)
    return dict(tokens=tokens, learning_rate=learning_rate, weight_in=weight_in, grad_in=grad_in, moment_in=moment_in, second_in=second_in, weight_out=weight_out, grad_out=grad_out, moment_out=moment_out, second_out=second_out)


first_decay = 0.9
second_decay = 0.95
first_fix = 1.0 - 0.9 ** 20
second_fix = 1.0 - 0.95 ** 20
epsilon = 1e-08
gelu_coeff = math.sqrt(2.0 / math.pi)

def adam_direction(grad, moment, second, scale):
    grad_wide = grad.astype(jnp.float32)
    moment_new = first_decay * moment.astype(jnp.float32) + (1.0 - first_decay) * grad_wide
    second_new = second_decay * second.astype(jnp.float32) + (1.0 - second_decay) * grad_wide * grad_wide
    return -scale * (moment_new / first_fix) / (jnp.sqrt(second_new / second_fix) + epsilon)

def activate(hidden_pair, width):
    hidden = hidden_pair[:, :width]
    hidden_tan = hidden_pair[:, width:]
    inner = gelu_coeff * (hidden + 0.044715 * hidden * hidden * hidden)
    shaped = jnp.tanh(inner)
    value = 0.5 * hidden * (1.0 + shaped)
    slope = 0.5 * (1.0 + shaped) + 0.5 * hidden * (1.0 - shaped * shaped) * gelu_coeff * (1.0 + 3.0 * 0.044715 * hidden * hidden)
    return (value.astype(jnp.bfloat16), (slope * hidden_tan).astype(jnp.bfloat16))

def reference(tokens, learning_rate, weight_in, grad_in, moment_in, second_in, weight_out, grad_out, moment_out, second_out):
    rate = learning_rate[0]
    dir_in = adam_direction(grad_in, moment_in, second_in, 1.0 / math.sqrt(D))
    new_in = (weight_in.astype(jnp.float32) + rate * dir_in).astype(jnp.bfloat16)
    delta_in = dir_in.astype(jnp.bfloat16)
    dir_out = adam_direction(grad_out, moment_out, second_out, 1.0 / math.sqrt(FF))
    new_out = (weight_out.astype(jnp.float32) + rate * dir_out).astype(jnp.bfloat16)
    delta_out = dir_out.astype(jnp.bfloat16)
    block_d = D // N_ROW
    block_f = FF // N_COL

    def first_block(index, total):
        begin = index * block_d
        rows_x = lax.dynamic_slice_in_dim(tokens, begin, block_d, 1)
        rows_w = lax.dynamic_slice_in_dim(new_in, begin, block_d, 0)
        rows_d = lax.dynamic_slice_in_dim(delta_in, begin, block_d, 0)
        part = jnp.concatenate([jnp.dot(rows_x, rows_w, preferred_element_type=jnp.float32), jnp.dot(rows_x, rows_d, preferred_element_type=jnp.float32)], axis=1)
        part = lax.optimization_barrier(part.astype(jnp.bfloat16))
        return total + part.astype(jnp.float32)
    hidden_pair = lax.fori_loop(0, N_ROW, first_block, jnp.zeros((TOKENS, 2 * FF), jnp.float32))
    value, tangent = activate(hidden_pair, FF)

    def second_block(index, total):
        begin = index * block_f
        cols_v = lax.dynamic_slice_in_dim(value, begin, block_f, 1)
        cols_t = lax.dynamic_slice_in_dim(tangent, begin, block_f, 1)
        rows_w = lax.dynamic_slice_in_dim(new_out, begin, block_f, 0)
        rows_d = lax.dynamic_slice_in_dim(delta_out, begin, block_f, 0)
        primal = jnp.dot(cols_v, rows_w, preferred_element_type=jnp.float32)
        along = jnp.dot(cols_t, rows_w, preferred_element_type=jnp.float32) + jnp.dot(cols_v, rows_d, preferred_element_type=jnp.float32)
        part = jnp.concatenate([primal, along], axis=1)
        part = lax.optimization_barrier(part.astype(jnp.bfloat16))
        return total + part.astype(jnp.float32)
    out_pair = lax.fori_loop(0, N_COL, second_block, jnp.zeros((TOKENS, 2 * D), jnp.float32))
    return (out_pair[:, :D].astype(jnp.bfloat16), out_pair[:, D:].astype(jnp.bfloat16))
```

```python
import functools
import math

import jax
import jax.numpy as jnp
from jax import lax
from jax.experimental import pallas as pl
from jax.experimental.pallas import tpu as pltpu
from jax.sharding import PartitionSpec as P


first_decay = 0.9
second_decay = 0.95
first_fix = 1.0 - 0.9**20
second_fix = 1.0 - 0.95**20
epsilon = 1e-08
gelu_coeff = math.sqrt(2.0 / math.pi)

GROUPS = 4
TILES = 6
SUBS = 6
SLOTS = 8
F32 = jnp.float32
BF16 = jnp.bfloat16


def activate(hidden, hidden_tan):
    inner = gelu_coeff * (hidden + 0.044715 * hidden * hidden * hidden)
    shaped = jnp.tanh(inner)
    value = 0.5 * hidden * (1.0 + shaped)
    slope = 0.5 * (1.0 + shaped) + 0.5 * hidden * (1.0 - shaped * shaped) * gelu_coeff * (
        1.0 + 3.0 * 0.044715 * hidden * hidden
    )
    return value.astype(BF16), (slope * hidden_tan).astype(BF16)


def loop(n, body):
    def step(i, carry):
        body(i)
        return carry

    lax.fori_loop(0, n, step, 0)


def kernel(
    nr,
    nc,
    tl,
    dl,
    fl,
    tokens,
    rate_ref,
    w_in,
    g_in,
    m_in,
    v_in,
    w_out,
    g_out,
    m_out,
    v_out,
    out_ref,
    tan_ref,
    weights,
    tok,
    part,
    got,
    acc,
    core_got,
    z_got,
    stream,
    stream_sem,
    own_sem,
    tok_send,
    tok_recv,
    fwd_send,
    fwd_recv,
    rs_send,
    rs_recv,
    ag_send,
    ag_recv,
    core_send,
    core_recv,
    z_send,
    z_recv,
):
    bits = nr.bit_length() - 1
    chips = nc // 2
    cpg = chips // GROUPS
    gr = cpg * 2 * tl
    pr = gr // nr
    tw = fl // TILES
    sr = dl // SUBS
    half = nr // 2
    npz = tl // pr
    per = dl // tw
    row = lax.axis_index("row")
    col = lax.axis_index("col")
    core, chip = lax.rem(col, 2), lax.div(col, 2)
    mine, zi_me = lax.div(chip, cpg), lax.rem(chip, cpg)
    order = (list(range(bits)), list(range(bits))[::-1])
    rate = rate_ref[0]

    def bit_of(b):
        return lax.rem(lax.div(row, 1 << b), 2)

    def across(b):
        return {"row": row + (1 - 2 * bit_of(b)) * (1 << b)}

    partner = {"col": col + 1 - 2 * core}

    def place(s, r):
        return sum(((r >> o) & 1) << (bits - 1 - k) for k, o in enumerate(order[s]))

    def my_place(s):
        return sum(bit_of(o) * (1 << (bits - 1 - k)) for k, o in enumerate(order[s]))

    here = (my_place(0), my_place(1))

    def keep_at(s, k):
        n = nr >> (k + 1)
        return lax.div(here[s], n) * n

    def send_at(s, k):
        n = nr >> (k + 1)
        return keep_at(s, k) + n * (1 - 2 * lax.rem(lax.div(here[s], n), 2))

    def remote(src, dst, send, recv, device):
        return pltpu.make_async_remote_copy(
            src_ref=src,
            dst_ref=dst,
            send_sem=send,
            recv_sem=recv,
            device_id=device,
            device_id_type=pl.DeviceIdType.MESH,
        )

    def others(p):
        if isinstance(p, int) and p == 0:
            return [lax.rem(zi_me + e, cpg) for e in range(1, cpg)]
        return list(range(cpg))

    def device_at(p, zi):
        return {"col": (lax.rem(mine + p, GROUPS) * cpg + zi) * 2 + core}


    ins = (w_in, g_in, m_in, v_in)
    outs = (w_out, g_out, m_out, v_out)
    count = TILES * SUBS

    def fetch(q, side):
        slot = lax.rem(q, SLOTS)
        q = lax.rem(q, count)
        b, i = lax.div(q, SUBS), lax.rem(q, SUBS)
        if side == 0:
            r0, c0 = i * sr, b * tw
        else:
            r0, c0 = lax.div(b, per) * dl + i * sr, lax.rem(b, per) * tw
        window = (pl.ds(pl.multiple_of(r0, sr), sr), pl.ds(pl.multiple_of(c0, tw), tw))
        return [
            pltpu.make_async_copy(ref.at[window], stream.at[slot, a], stream_sem.at[slot, a])
            for a, ref in enumerate((ins, outs)[side])
        ]

    def fetch_start(q):
        @pl.when(q < count)
        def _():
            for copy in fetch(q, 0):
                copy.start()

        @pl.when(jnp.logical_and(q >= count, q < 2 * count))
        def _():
            for copy in fetch(q, 1):
                copy.start()

    step_rows = 16

    def adam_block(b, side):
        scale = 1.0 / math.sqrt((dl * nr, fl * nc)[side])

        def sub(i):
            q = side * count + b * SUBS + i
            slot = lax.rem(q, SLOTS)
            for copy in fetch(q, side):
                copy.wait()

            def rows(t):
                at = pl.ds(pl.multiple_of(t * step_rows, step_rows), step_rows)
                to = pl.ds(pl.multiple_of(i * sr + t * step_rows, step_rows), step_rows)
                w, g, m, v = (stream[slot, a, at, :].astype(F32) for a in range(4))
                top = (-scale * first_decay / first_fix) * m + (
                    -scale * (1.0 - first_decay) / first_fix
                ) * g
                under = (second_decay / second_fix) * v + (
                    (1.0 - second_decay) / second_fix
                ) * (g * g)
                direction = top / (under * lax.rsqrt(under) + epsilon)
                weights[0, b, to, :] = (w + rate * direction).astype(BF16)
                weights[1, b, to, :] = direction.astype(BF16)

            loop(sr // step_rows, rows)
            fetch_start(q + SLOTS)

        loop(SUBS, sub)


    def tok_rows(zi):
        return pl.ds(pl.multiple_of(zi * tl, tl), tl)

    own_copy = pltpu.make_async_copy(tokens, tok.at[0, core, tok_rows(zi_me)], own_sem)

    def tok_copy(p, zi):
        back = (GROUPS - p) % GROUPS
        return remote(
            tokens,
            tok.at[back, core, tok_rows(zi_me)],
            tok_send.at[p, zi],
            tok_recv.at[back, zi_me],
            device_at(p, zi),
        )

    def tok_arrive(p, zi):
        return remote(
            tokens,
            tok.at[p, core, tok_rows(zi)],
            tok_send.at[p, zi],
            tok_recv.at[p, zi],
            partner,
        )

    def forward(p, zi, own=False):
        src = tokens if own else tok.at[p, core, tok_rows(zi)]
        return remote(
            src, tok.at[p, core, tok_rows(zi)], fwd_send.at[p, zi], fwd_recv.at[p, zi], partner
        )

    def forward_arrive(p, zi):
        return remote(
            tokens, tok.at[p, 1 - core, tok_rows(zi)], fwd_send.at[p, zi], fwd_recv.at[p, zi], partner
        )

    def forward_group(p):
        for zi in others(p):
            tok_arrive(p, zi).wait_recv()
            forward(p, zi).start()

    def await_group(p):
        for zi in range(cpg):
            forward_arrive(p, zi).wait_recv()


    def m1(p, j):
        lhs = tok[p].reshape(gr, dl)
        for s in range(2):
            block = jnp.dot(lhs, weights[s, j], preferred_element_type=F32).astype(BF16)
            for q in range(nr):
                part[p, s, j, place(s, q)] = block[q * pr : (q + 1) * pr]

    def rs_copy(s, k, p, j):
        n = nr >> (k + 1)
        return remote(
            part.at[p, s, j, pl.ds(send_at(s, k), n)],
            got.at[p, s, j, pl.ds(nr - (nr >> k), n)],
            rs_send.at[p, j, s, k],
            rs_recv.at[p, j, s, k],
            across(order[s][k]),
        )

    def rs_first(p, j):
        for s in range(2):
            rs_copy(s, 0, p, j).start()

    def rs_mid(p, j):
        for k in range(1, bits):
            n = nr >> k
            for s in range(2):
                rs_copy(s, k - 1, p, j).wait()
                at = pl.ds(keep_at(s, k - 1), n)
                part[p, s, j, at] = (
                    part[p, s, j, at].astype(F32)
                    + got[p, s, j, nr - (nr >> (k - 1)) : nr - (nr >> k)].astype(F32)
                ).astype(BF16)
            for s in range(2):
                rs_copy(s, k, p, j).start()

    def ag_landing(s, k, p, j, at):
        n = nr >> (k + 1)
        if k == 0:
            return part.at[p, s, j, at]
        return got.at[p, s, j, pl.ds(half - (nr >> k), n)]

    def ag_copy(s, k, p, j):
        at = pl.ds(keep_at(s, k), nr >> (k + 1))
        return remote(
            part.at[p, s, j, at],
            ag_landing(s, k, p, j, at),
            ag_send.at[p, j, s, k],
            ag_recv.at[p, j, s, k],
            across(order[s][k]),
        )

    def ag_arrive(s, k, p, j):
        at = pl.ds(send_at(s, k), nr >> (k + 1))
        return remote(
            part.at[p, s, j, at],
            ag_landing(s, k, p, j, at),
            ag_send.at[p, j, s, k],
            ag_recv.at[p, j, s, k],
            across(order[s][k]),
        )

    def act(p, j):
        sums = []
        for s in range(2):
            rs_copy(s, bits - 1, p, j).wait()
            sums.append(part[p, s, j, here[s]].astype(F32) + got[p, s, j, nr - 2].astype(F32))
        for s, block in enumerate(activate(*sums)):
            part[p, s, j, here[s]] = block
        for s in range(2):
            ag_copy(s, bits - 1, p, j).start()

    def ag_mid(p, j):
        for k in range(bits - 2, -1, -1):
            for s in range(2):
                ag_arrive(s, k + 1, p, j).wait_recv()
                n = nr >> (k + 2)
                off = half - (nr >> (k + 1))
                part[p, s, j, pl.ds(send_at(s, k + 1), n)] = got[p, s, j, off : off + n]
            for s in range(2):
                ag_copy(s, k, p, j).start()


    def m2(p, j):
        for s in range(2):
            ag_arrive(s, 0, p, j).wait_recv()
        value, tangent = (
            jnp.concatenate([part[p, s, j, place(s, q)] for q in range(nr)], axis=0)
            for s in range(2)
        )
        base = lax.div(j, per) * per
        at = pl.ds(pl.multiple_of(lax.rem(j, per) * tw, tw), tw)
        for n in range(per):
            new, delta = weights[0, base + n, at, :], weights[1, base + n, at, :]
            acc[0, n] += jnp.dot(value, new, preferred_element_type=F32)
            acc[1, n] += jnp.dot(tangent, new, preferred_element_type=F32) + jnp.dot(
                value, delta, preferred_element_type=F32
            )

    def core_copy(p, n):
        at = pl.ds((1 - core) * half, half)
        return remote(
            part.at[p, 0, pl.ds(2 * n, 2), at],
            core_got.at[p, pl.ds(2 * n, 2)],
            core_send.at[p, n],
            core_recv.at[p, n],
            partner,
        )

    def z_copy(p, zi, back):
        return remote(
            part.at[p, 0, :, pl.ds(core * half + zi * npz, npz)],
            z_got.at[back, zi_me],
            z_send.at[p, zi],
            z_recv.at[back, zi_me],
            device_at(p, zi),
        )

    def z_arrive(p, zi):
        return remote(
            part.at[0, 0, :, pl.ds(core * half + zi_me * npz, npz)],
            z_got.at[p, zi],
            z_send.at[p, zi],
            z_recv.at[p, zi],
            partner,
        )

    def finish(p):
        def drain(j):
            for s in range(2):
                for k in range(bits):
                    ag_copy(s, k, p, j).wait_send()

        loop(TILES, drain)
        for n in range(per):
            for t in range(2):
                part[p, 0, 2 * n + t] = acc[t, n].astype(BF16).reshape(nr, pr, tw)
            core_copy(p, n).start()
        at = pl.ds(core * half, half)
        for n in range(per):
            core_copy(p, n).wait()
            for t in (2 * n, 2 * n + 1):
                part[p, 0, t, at] = (
                    part[p, 0, t, at].astype(F32) + core_got[p, t].astype(F32)
                ).astype(BF16)


    loop(SLOTS, fetch_start)
    own_copy.start()
    barrier = pltpu.get_barrier_semaphore()
    near = [across(b) for b in range(bits)] + [partner]
    near += [device_at(p, zi) for p in range(GROUPS) for zi in others(p)]
    for device in near:
        pl.semaphore_signal(
            barrier, inc=1, device_id=device, device_id_type=pl.DeviceIdType.MESH
        )
    pl.semaphore_wait(barrier, len(near))
    forward(0, zi_me, own=True).start()
    for p in list(range(GROUPS))[::-1]:
        for zi in others(p):
            tok_copy(p, zi).start()

    def phase_a(j):
        adam_block(j, 0)

        @pl.when(j == 0)
        def _():
            own_copy.wait()
            forward_group(0)
            await_group(0)

        m1(0, j)
        rs_first(0, j)

        @pl.when(j >= 1)
        def _():
            rs_mid(0, j - 1)

        for p in range(1, GROUPS):

            @pl.when(j == TILES - GROUPS + p)
            def _(p=p):
                forward_group(p)

    loop(TILES, phase_a)

    def phase_b(u):
        p, j = 1 + lax.div(u, TILES), lax.rem(u, TILES)

        @pl.when(j == 0)
        def _():
            await_group(p)

        m1(p, j)
        rs_first(p, j)

        @pl.when(u == 2)
        def _():
            rs_mid(0, TILES - 1)

    loop((GROUPS - 1) * TILES, phase_b)

    def phase_c(b):
        adam_block(b, 1)

        def mids(t):
            u = b * (GROUPS - 1) + t
            rs_mid(1 + lax.div(u, TILES), lax.rem(u, TILES))

        loop(GROUPS - 1, mids)
        act(0, b)

    loop(TILES, phase_c)

    def acts(u):
        act(1 + lax.div(u, TILES), lax.rem(u, TILES))

    loop(2 * TILES, acts)
    loop(TILES, lambda j: ag_mid(1, j))
    loop(TILES, lambda j: act(3, j))
    loop(TILES, lambda j: ag_mid(2, j))

    def phase_d(i):
        p = lax.rem(i + 1, GROUPS)
        acc[...] = jnp.zeros_like(acc)
        loop(TILES, lambda j: m2(p, j))
        finish(p)

        @pl.when(i < GROUPS - 1)
        def _():
            for zi in range(cpg):
                z_copy(p, zi, GROUPS - p).start()

        @pl.when(i < 2)
        def _():
            loop(TILES, lambda j: ag_mid(lax.rem(i + 3, GROUPS), j))

    loop(GROUPS, phase_d)
    for zi in others(0):
        z_copy(0, zi, 0).start()
    sources = [(p, zi) for p in range(GROUPS) for zi in others(p)]
    for p, zi in sources:
        z_arrive(p, zi).wait_recv()
    at = pl.ds(core * half + zi_me * npz, npz)
    for t in range(2 * per):
        total = part[0, 0, t, at].astype(F32)
        for p, zi in sources:
            total += z_got[p, zi, t].astype(F32)
        ref = (out_ref, tan_ref)[t % 2]
        ref[:, (t // 2) * tw : (t // 2 + 1) * tw] = total.reshape(tl, tw).astype(BF16)
    for p in range(GROUPS):
        for zi in range(cpg):
            if p > 0:
                forward(p, zi).wait_send()
        for zi in others(p):
            tok_copy(p, zi).wait_send()
            z_copy(p, zi, (GROUPS - p) % GROUPS).wait_send()
    forward(0, zi_me, own=True).wait_send()
    for zi in others(0):
        forward(0, zi).wait_send()


def make_body(nr, nc):
    bits = nr.bit_length() - 1
    chips = nc // 2

    def body(tokens, learning_rate, *arrays):
        dl, fl = arrays[0].shape
        tl = tokens.shape[0]
        cpg = chips // GROUPS
        gr = cpg * 2 * tl
        pr = gr // nr
        tw = fl // TILES
        half = nr // 2
        npz = tl // pr
        sem = pltpu.SemaphoreType.DMA
        hbm = pl.BlockSpec(memory_space=pl.ANY)
        vmem = pl.BlockSpec(memory_space=pltpu.VMEM)
        return pl.pallas_call(
            functools.partial(kernel, nr, nc, tl, dl, fl),
            out_shape=[jax.ShapeDtypeStruct((tl, dl), BF16)] * 2,
            in_specs=[hbm, pl.BlockSpec(memory_space=pltpu.SMEM)] + [hbm] * 8,
            out_specs=[vmem, vmem],
            scratch_shapes=[
                pltpu.VMEM((2, TILES, dl, tw), BF16),
                pltpu.VMEM((GROUPS, 2, cpg * tl, dl), BF16),
                pltpu.VMEM((GROUPS, 2, TILES, nr, pr, tw), BF16),
                pltpu.VMEM((GROUPS, 2, TILES, nr - 1, pr, tw), BF16),
                pltpu.VMEM((2, dl // tw, gr, tw), F32),
                pltpu.VMEM((GROUPS, 2 * dl // tw, half, pr, tw), BF16),
                pltpu.VMEM((GROUPS, cpg, 2 * dl // tw, npz, pr, tw), BF16),
                pltpu.VMEM((SLOTS, 4, dl // SUBS, tw), BF16),
                sem((SLOTS, 4)),
                sem,
                sem((GROUPS, cpg)),
                sem((GROUPS, cpg)),
                sem((GROUPS, cpg)),
                sem((GROUPS, cpg)),
                sem((GROUPS, TILES, 2, bits)),
                sem((GROUPS, TILES, 2, bits)),
                sem((GROUPS, TILES, 2, bits)),
                sem((GROUPS, TILES, 2, bits)),
                sem((GROUPS, dl // tw)),
                sem((GROUPS, dl // tw)),
                sem((GROUPS, cpg)),
                sem((GROUPS, cpg)),
            ],
            compiler_params=pltpu.CompilerParams(
                collective_id=0, has_side_effects=True, vmem_limit_bytes=67043328
            ),
        )(tokens, learning_rate, *arrays)

    return body


def solution(mesh):
    nr, nc = mesh.shape["row"], mesh.shape["col"]
    return jax.shard_map(
        make_body(nr, nc),
        mesh=mesh,
        in_specs=(
            P("col", "row"),
            P(),
            P("row", "col"),
            P("row", "col"),
            P("row", "col"),
            P("row", "col"),
            P("col", "row"),
            P("col", "row"),
            P("col", "row"),
            P("col", "row"),
        ),
        out_specs=(P("col", "row"), P("col", "row")),
        check_vma=False,
    )
```

```python
import functools
import math

import jax
import jax.numpy as jnp
from jax import lax
from jax.experimental import pallas as pl
from jax.experimental.pallas import tpu as pltpu
from jax.sharding import PartitionSpec as P


first_decay = 0.9
second_decay = 0.95
first_fix = 1.0 - 0.9**20
second_fix = 1.0 - 0.95**20
epsilon = 1e-08
gelu_coeff = math.sqrt(2.0 / math.pi)

GROUPS = 4
TILES = 6
SUBS = 6
SLOTS = 8
LAG = 1
F32 = jnp.float32
BF16 = jnp.bfloat16


def activate(hidden, hidden_tan):
    inner = gelu_coeff * (hidden + 0.044715 * hidden * hidden * hidden)
    shaped = jnp.tanh(inner)
    value = 0.5 * hidden * (1.0 + shaped)
    slope = 0.5 * (1.0 + shaped) + 0.5 * hidden * (1.0 - shaped * shaped) * gelu_coeff * (
        1.0 + 3.0 * 0.044715 * hidden * hidden
    )
    return value.astype(BF16), (slope * hidden_tan).astype(BF16)


def loop(n, body):
    def step(i, carry):
        body(i)
        return carry

    lax.fori_loop(0, n, step, 0)


def kernel(
    nr,
    nc,
    tl,
    dl,
    fl,
    tokens,
    rate_ref,
    w_in,
    g_in,
    m_in,
    v_in,
    w_out,
    g_out,
    m_out,
    v_out,
    out_ref,
    tan_ref,
    weights,
    tok,
    part,
    got,
    acc,
    core_got,
    z_got,
    stream,
    stream_sem,
    own_sem,
    tok_send,
    tok_recv,
    fwd_send,
    fwd_recv,
    rs_send,
    rs_recv,
    ag_send,
    ag_recv,
    core_send,
    core_recv,
    z_send,
    z_recv,
):
    bits = nr.bit_length() - 1
    chips = nc // 2
    cpg = chips // GROUPS
    gr = cpg * 2 * tl
    pr = gr // nr
    tw = fl // TILES
    sr = dl // SUBS
    half = nr // 2
    npz = tl // pr
    per = dl // tw
    row = lax.axis_index("row")
    col = lax.axis_index("col")
    core, chip = lax.rem(col, 2), lax.div(col, 2)
    mine, zi_me = lax.div(chip, cpg), lax.rem(chip, cpg)
    order = (list(range(bits)), list(range(bits))[::-1])
    rate = rate_ref[0]

    def bit_of(b):
        return lax.rem(lax.div(row, 1 << b), 2)

    def across(b):
        return {"row": row + (1 - 2 * bit_of(b)) * (1 << b)}

    partner = {"col": col + 1 - 2 * core}

    def place(s, r):
        return sum(((r >> o) & 1) << (bits - 1 - k) for k, o in enumerate(order[s]))

    def my_place(s):
        return sum(bit_of(o) * (1 << (bits - 1 - k)) for k, o in enumerate(order[s]))

    here = (my_place(0), my_place(1))

    def keep_at(s, k):
        n = nr >> (k + 1)
        return lax.div(here[s], n) * n

    def send_at(s, k):
        n = nr >> (k + 1)
        return keep_at(s, k) + n * (1 - 2 * lax.rem(lax.div(here[s], n), 2))

    def remote(src, dst, send, recv, device):
        return pltpu.make_async_remote_copy(
            src_ref=src,
            dst_ref=dst,
            send_sem=send,
            recv_sem=recv,
            device_id=device,
            device_id_type=pl.DeviceIdType.MESH,
        )

    def others(p):
        if isinstance(p, int) and p == 0:
            return [lax.rem(zi_me + e, cpg) for e in range(1, cpg)]
        return list(range(cpg))

    def device_at(p, zi):
        return {"col": (lax.rem(mine + p, GROUPS) * cpg + zi) * 2 + core}


    ins = (w_in, g_in, m_in, v_in)
    outs = (w_out, g_out, m_out, v_out)
    count = TILES * SUBS

    def fetch(q, side):
        slot = lax.rem(q, SLOTS)
        q = lax.rem(q, count)
        b, i = lax.div(q, SUBS), lax.rem(q, SUBS)
        if side == 0:
            r0, c0 = i * sr, b * tw
        else:
            r0, c0 = lax.div(b, per) * dl + i * sr, lax.rem(b, per) * tw
        window = (pl.ds(pl.multiple_of(r0, sr), sr), pl.ds(pl.multiple_of(c0, tw), tw))
        return [
            pltpu.make_async_copy(ref.at[window], stream.at[slot, a], stream_sem.at[slot, a])
            for a, ref in enumerate((ins, outs)[side])
        ]

    def fetch_start(q):
        @pl.when(q < count)
        def _():
            for copy in fetch(q, 0):
                copy.start()

        @pl.when(jnp.logical_and(q >= count, q < 2 * count))
        def _():
            for copy in fetch(q, 1):
                copy.start()

    step_rows = 16

    def adam_sub(at_sub, side):
        scale = 1.0 / math.sqrt((dl * nr, fl * nc)[side])
        b, i = lax.div(at_sub, SUBS), lax.rem(at_sub, SUBS)
        q = side * count + at_sub
        slot = lax.rem(q, SLOTS)
        for copy in fetch(q, side):
            copy.wait()

        def rows(t):
            at = pl.ds(pl.multiple_of(t * step_rows, step_rows), step_rows)
            to = pl.ds(pl.multiple_of(i * sr + t * step_rows, step_rows), step_rows)
            w, g, m, v = (stream[slot, a, at, :].astype(F32) for a in range(4))
            top = (-scale * first_decay / first_fix) * m + (
                -scale * (1.0 - first_decay) / first_fix
            ) * g
            under = (second_decay / second_fix) * v + (
                (1.0 - second_decay) / second_fix
            ) * (g * g)
            direction = top / (under * lax.rsqrt(under) + epsilon)
            weights[0, b, to, :] = (w + rate * direction).astype(BF16)
            weights[1, b, to, :] = direction.astype(BF16)

        loop(sr // step_rows, rows)
        fetch_start(q + SLOTS)


    def tok_rows(zi):
        return pl.ds(pl.multiple_of(zi * tl, tl), tl)

    own_copy = pltpu.make_async_copy(tokens, tok.at[0, core, tok_rows(zi_me)], own_sem)

    def tok_copy(p, zi):
        back = (GROUPS - p) % GROUPS
        return remote(
            tokens,
            tok.at[back, core, tok_rows(zi_me)],
            tok_send.at[p, zi],
            tok_recv.at[back, zi_me],
            device_at(p, zi),
        )

    def tok_arrive(p, zi):
        return remote(
            tokens,
            tok.at[p, core, tok_rows(zi)],
            tok_send.at[p, zi],
            tok_recv.at[p, zi],
            partner,
        )

    def forward(p, zi, own=False):
        src = tokens if own else tok.at[p, core, tok_rows(zi)]
        return remote(
            src, tok.at[p, core, tok_rows(zi)], fwd_send.at[p, zi], fwd_recv.at[p, zi], partner
        )

    def forward_arrive(p, zi):
        return remote(
            tokens, tok.at[p, 1 - core, tok_rows(zi)], fwd_send.at[p, zi], fwd_recv.at[p, zi], partner
        )

    def forward_group(p):
        for zi in others(p):
            tok_arrive(p, zi).wait_recv()
            forward(p, zi).start()

    def await_group(p):
        for zi in range(cpg):
            forward_arrive(p, zi).wait_recv()


    def m1(p, j):
        lhs = tok[p].reshape(gr, dl)
        for s in range(2):
            block = jnp.dot(lhs, weights[s, j], preferred_element_type=F32).astype(BF16)
            for q in range(nr):
                part[p, s, j, place(s, q)] = block[q * pr : (q + 1) * pr]

    def rs_copy(s, k, p, j):
        n = nr >> (k + 1)
        return remote(
            part.at[p, s, j, pl.ds(send_at(s, k), n)],
            got.at[p, s, j, pl.ds(nr - (nr >> k), n)],
            rs_send.at[p, j, s, k],
            rs_recv.at[p, j, s, k],
            across(order[s][k]),
        )

    def rs_first(p, j):
        for s in range(2):
            rs_copy(s, 0, p, j).start()

    def rs_mid(p, j):
        for k in range(1, bits):
            n = nr >> k
            for s in range(2):
                rs_copy(s, k - 1, p, j).wait()
                at = pl.ds(keep_at(s, k - 1), n)
                part[p, s, j, at] = (
                    part[p, s, j, at].astype(F32)
                    + got[p, s, j, nr - (nr >> (k - 1)) : nr - (nr >> k)].astype(F32)
                ).astype(BF16)
            for s in range(2):
                rs_copy(s, k, p, j).start()

    def ag_landing(s, k, p, j, at):
        n = nr >> (k + 1)
        if k == 0:
            return part.at[p, s, j, at]
        return got.at[p, s, j, pl.ds(half - (nr >> k), n)]

    def ag_copy(s, k, p, j):
        at = pl.ds(keep_at(s, k), nr >> (k + 1))
        return remote(
            part.at[p, s, j, at],
            ag_landing(s, k, p, j, at),
            ag_send.at[p, j, s, k],
            ag_recv.at[p, j, s, k],
            across(order[s][k]),
        )

    def ag_arrive(s, k, p, j):
        at = pl.ds(send_at(s, k), nr >> (k + 1))
        return remote(
            part.at[p, s, j, at],
            ag_landing(s, k, p, j, at),
            ag_send.at[p, j, s, k],
            ag_recv.at[p, j, s, k],
            across(order[s][k]),
        )

    def act(p, j):
        sums = []
        for s in range(2):
            rs_copy(s, bits - 1, p, j).wait()
            sums.append(part[p, s, j, here[s]].astype(F32) + got[p, s, j, nr - 2].astype(F32))
        for s, block in enumerate(activate(*sums)):
            part[p, s, j, here[s]] = block
        for s in range(2):
            ag_copy(s, bits - 1, p, j).start()

    def ag_mid(p, j):
        for k in range(bits - 2, -1, -1):
            for s in range(2):
                ag_arrive(s, k + 1, p, j).wait_recv()
                n = nr >> (k + 2)
                off = half - (nr >> (k + 1))
                part[p, s, j, pl.ds(send_at(s, k + 1), n)] = got[p, s, j, off : off + n]
            for s in range(2):
                ag_copy(s, k, p, j).start()


    def m2(p, j):
        for s in range(2):
            ag_arrive(s, 0, p, j).wait_recv()
        value, tangent = (
            jnp.concatenate([part[p, s, j, place(s, q)] for q in range(nr)], axis=0)
            for s in range(2)
        )
        base = lax.div(j, per) * per
        at = pl.ds(pl.multiple_of(lax.rem(j, per) * tw, tw), tw)
        for n in range(per):
            new, delta = weights[0, base + n, at, :], weights[1, base + n, at, :]
            acc[0, n] += jnp.dot(value, new, preferred_element_type=F32)
            acc[1, n] += jnp.dot(tangent, new, preferred_element_type=F32) + jnp.dot(
                value, delta, preferred_element_type=F32
            )

    def core_copy(p, n):
        at = pl.ds((1 - core) * half, half)
        return remote(
            part.at[p, 0, pl.ds(2 * n, 2), at],
            core_got.at[p, pl.ds(2 * n, 2)],
            core_send.at[p, n],
            core_recv.at[p, n],
            partner,
        )

    def z_copy(p, zi, back):
        return remote(
            part.at[p, 0, :, pl.ds(core * half + zi * npz, npz)],
            z_got.at[back, zi_me],
            z_send.at[p, zi],
            z_recv.at[back, zi_me],
            device_at(p, zi),
        )

    def z_arrive(p, zi):
        return remote(
            part.at[0, 0, :, pl.ds(core * half + zi_me * npz, npz)],
            z_got.at[p, zi],
            z_send.at[p, zi],
            z_recv.at[p, zi],
            partner,
        )

    def finish(p):
        def drain(j):
            for s in range(2):
                for k in range(bits):
                    ag_copy(s, k, p, j).wait_send()

        loop(TILES, drain)
        for n in range(per):
            for t in range(2):
                part[p, 0, 2 * n + t] = acc[t, n].astype(BF16).reshape(nr, pr, tw)
            core_copy(p, n).start()
        at = pl.ds(core * half, half)
        for n in range(per):
            core_copy(p, n).wait()
            for t in (2 * n, 2 * n + 1):
                part[p, 0, t, at] = (
                    part[p, 0, t, at].astype(F32) + core_got[p, t].astype(F32)
                ).astype(BF16)


    loop(SLOTS, fetch_start)
    own_copy.start()
    barrier = pltpu.get_barrier_semaphore()
    near = [across(b) for b in range(bits)] + [partner]
    near += [device_at(p, zi) for p in range(GROUPS) for zi in others(p)]
    for device in near:
        pl.semaphore_signal(
            barrier, inc=1, device_id=device, device_id_type=pl.DeviceIdType.MESH
        )
    pl.semaphore_wait(barrier, len(near))
    forward(0, zi_me, own=True).start()
    for p in list(range(GROUPS))[::-1]:
        for zi in others(p):
            tok_copy(p, zi).start()

    def unit(u):
        return lax.rem(lax.div(u, TILES), GROUPS), lax.rem(u, TILES)

    def phase_a(j):
        loop(SUBS, lambda i: adam_sub(j * SUBS + i, 0))

        @pl.when(j == 0)
        def _():
            own_copy.wait()
            forward_group(0)
            await_group(0)

        m1(0, j)
        rs_first(0, j)

        @pl.when(j >= 1)
        def _():
            rs_mid(0, j - 1)

        @pl.when(j >= 2)
        def _():
            act(0, j - 2)

        @pl.when(j == TILES - 2)
        def _():
            forward_group(1)

    loop(TILES, phase_a)
    await_group(1)
    m1(1, 0)
    units = GROUPS * TILES

    def m1_unit(u):
        p, j = unit(u)

        @pl.when(u < units)
        def _():
            @pl.when(j == 0)
            def _():
                await_group(p)

            m1(p, j)

    def m2_unit(u):
        p, j = unit(u)

        @pl.when(j == 0)
        def _():
            acc[...] = jnp.zeros_like(acc)

        m2(p, j)

        @pl.when(j == TILES - 1)
        def _():
            finish(p)

            @pl.when(p > 0)
            def _():
                for zi in range(cpg):
                    z_copy(p, zi, GROUPS - p).start()

    def tick(step):
        t = step + TILES

        @pl.when(t < units)
        def _():
            rs_first(*unit(t))

        @pl.when(step == 0)
        def _():
            rs_mid(*unit(TILES - 1))

        @pl.when(step < 2)
        def _():
            act(*unit(t - 2))

        for at, stage in ((t - LAG, rs_mid), (t - 2 * LAG, act), (t - 3 * LAG, ag_mid)):

            @pl.when(jnp.logical_and(at >= TILES, at < units))
            def _(at=at, stage=stage):
                stage(*unit(at))

        for p in range(2, GROUPS):

            @pl.when(step == p - 2)
            def _(p=p):
                forward_group(p)

        @pl.when(step < 3)
        def _():
            loop(TILES, lambda k: m1_unit(TILES + 1 + step * TILES + k))

        @pl.when(jnp.logical_and(step >= 3, step < 7))
        def _():
            loop(count // 4, lambda k: adam_sub((step - 3) * (count // 4) + k, 1))

        late = 3 * LAG + 1
        catch = 7 - late

        @pl.when(jnp.logical_and(step >= 7, step < 7 + catch))
        def _():
            loop(2, lambda k: m2_unit(TILES + 2 * (step - 7) + k))

        @pl.when(step >= 7 + catch)
        def _():
            m2_unit(t - late)

    loop(units - TILES + 3 * LAG, tick)
    loop(TILES, lambda j: ag_mid(0, j))
    loop(TILES + 1, lambda k: m2_unit(units - 1 + k))
    for zi in others(0):
        z_copy(0, zi, 0).start()
    sources = [(p, zi) for p in range(GROUPS) for zi in others(p)]
    for p, zi in sources:
        z_arrive(p, zi).wait_recv()
    at = pl.ds(core * half + zi_me * npz, npz)
    for t in range(2 * per):
        total = part[0, 0, t, at].astype(F32)
        for p, zi in sources:
            total += z_got[p, zi, t].astype(F32)
        ref = (out_ref, tan_ref)[t % 2]
        ref[:, (t // 2) * tw : (t // 2 + 1) * tw] = total.reshape(tl, tw).astype(BF16)
    for p in range(GROUPS):
        for zi in range(cpg):
            if p > 0:
                forward(p, zi).wait_send()
        for zi in others(p):
            tok_copy(p, zi).wait_send()
            z_copy(p, zi, (GROUPS - p) % GROUPS).wait_send()
    forward(0, zi_me, own=True).wait_send()
    for zi in others(0):
        forward(0, zi).wait_send()


def make_body(nr, nc):
    bits = nr.bit_length() - 1
    chips = nc // 2

    def body(tokens, learning_rate, *arrays):
        dl, fl = arrays[0].shape
        tl = tokens.shape[0]
        cpg = chips // GROUPS
        gr = cpg * 2 * tl
        pr = gr // nr
        tw = fl // TILES
        half = nr // 2
        npz = tl // pr
        sem = pltpu.SemaphoreType.DMA
        hbm = pl.BlockSpec(memory_space=pl.ANY)
        vmem = pl.BlockSpec(memory_space=pltpu.VMEM)
        return pl.pallas_call(
            functools.partial(kernel, nr, nc, tl, dl, fl),
            out_shape=[jax.ShapeDtypeStruct((tl, dl), BF16)] * 2,
            in_specs=[hbm, pl.BlockSpec(memory_space=pltpu.SMEM)] + [hbm] * 8,
            out_specs=[vmem, vmem],
            scratch_shapes=[
                pltpu.VMEM((2, TILES, dl, tw), BF16),
                pltpu.VMEM((GROUPS, 2, cpg * tl, dl), BF16),
                pltpu.VMEM((GROUPS, 2, TILES, nr, pr, tw), BF16),
                pltpu.VMEM((GROUPS, 2, TILES, nr - 1, pr, tw), BF16),
                pltpu.VMEM((2, dl // tw, gr, tw), F32),
                pltpu.VMEM((GROUPS, 2 * dl // tw, half, pr, tw), BF16),
                pltpu.VMEM((GROUPS, cpg, 2 * dl // tw, npz, pr, tw), BF16),
                pltpu.VMEM((SLOTS, 4, dl // SUBS, tw), BF16),
                sem((SLOTS, 4)),
                sem,
                sem((GROUPS, cpg)),
                sem((GROUPS, cpg)),
                sem((GROUPS, cpg)),
                sem((GROUPS, cpg)),
                sem((GROUPS, TILES, 2, bits)),
                sem((GROUPS, TILES, 2, bits)),
                sem((GROUPS, TILES, 2, bits)),
                sem((GROUPS, TILES, 2, bits)),
                sem((GROUPS, dl // tw)),
                sem((GROUPS, dl // tw)),
                sem((GROUPS, cpg)),
                sem((GROUPS, cpg)),
            ],
            compiler_params=pltpu.CompilerParams(
                collective_id=0, has_side_effects=True, vmem_limit_bytes=67043328
            ),
        )(tokens, learning_rate, *arrays)

    return body


def solution(mesh):
    nr, nc = mesh.shape["row"], mesh.shape["col"]
    return jax.shard_map(
        make_body(nr, nc),
        mesh=mesh,
        in_specs=(
            P("col", "row"),
            P(),
            P("row", "col"),
            P("row", "col"),
            P("row", "col"),
            P("row", "col"),
            P("col", "row"),
            P("col", "row"),
            P("col", "row"),
            P("col", "row"),
        ),
        out_specs=(P("col", "row"), P("col", "row")),
        check_vma=False,
    )
```
